32 devices in a mesh: act: 4 (over x, core), fld: 8 (over z, y).
Axes of the slice: x: 2, y: 2, z: 4, core: 2. Of those that a mesh axis runs over, the one named last changes fastest.
Arguments:
- star_state: float32 [12, 32768], P(None, 'fld'), may hold values from -12 to 12
- star_times: float32 [32768], P('fld'), may hold values from -0.25 to 0
- masses: float32 [32768], P('fld'), may hold values from 6.1035155e-07 to 1.5258789e-05
- active_ids: int32 [4, 2048], replicated, may hold values from 0 to 32767, as said below
Outputs:
- final_state: float32 [12, 32768], P(None, 'fld')
- active_potentials: float32 [4, 2048], P(None, 'act')
The draws below stay inside these ranges and needn't reach their ends.
Inputs may be any that keep to these rules, and one draw needn't show every extreme that they name: `active_ids`: each row lists 2048 distinct star indices; the owners of the listed stars are uneven, with many listed stars in a few blocks of 4096 consecutive indices.
All inputs are finite; a program needn't handle non-finite values.
Results may differ from the reference program's by a relative error of at most 0.0001.
Values sent between devices are 32-bit elements; how exact they have to be, the bound alone decides.
A program may use at most 64 MiB of HBM per device.

```python
import math
import jax
import jax.numpy as jnp
from jax import lax

STAR_DEV = 4096
ACT_DEV = 512
STEPS = 4
N = 32768
N_ACT = 4
N_FLD = 8


def draw_star_state(key, part):
    star_total = STAR_DEV * N_FLD
    row_scales = jnp.array([0.1, 0.1, 0.1, 0.1, 0.1, 0.1, 0.5, 0.5, 0.5, 2.0, 2.0, 2.0], jnp.float32)[:, None]
    state_key = jax.random.fold_in(key, 11)
    unit = jnp.clip(jax.random.normal(state_key, (12, star_total), jnp.float32), -6.0, 6.0)
    return unit * row_scales


def draw_active_ids(key, part):
    star_total = STAR_DEV * N_FLD
    active_total = ACT_DEV * N_ACT

    def one_step(step_key):
        level_key, rank_key = jax.random.split(step_key)
        levels = jax.random.randint(level_key, (N_FLD,), 0, 4)
        ranking = jax.random.permutation(rank_key, star_total).astype(jnp.int32)
        owner_level = jnp.repeat(levels, STAR_DEV).astype(jnp.int32)
        scores = owner_level * star_total + ranking
        positions = jnp.arange(star_total, dtype=jnp.int32)
        scores = jnp.where((positions == 0) | (positions == star_total - 1), 5 * star_total, scores)
        chosen = lax.top_k(scores, active_total)[1]
        return chosen.astype(jnp.int32)
    step_keys = jax.random.split(jax.random.fold_in(key, 7), STEPS)
    return jax.vmap(one_step)(step_keys)


def steps_of(key, shape, pieces, smallest, largest):
    def one(axis_at, shards_of):
        draws = jax.random.uniform(jax.random.fold_in(jax.random.fold_in(key, 6), axis_at), (shards_of,), jnp.float32, smallest / len(pieces), largest / len(pieces))
        return jnp.repeat(jnp.exp(draws), shape[axis_at] // shards_of).reshape((-1,) + (1,) * (len(shape) - axis_at - 1))

    loudness = one(*pieces[0])
    for cut in pieces[1:]:
        loudness = loudness * one(*cut)
    return loudness


def setup_inputs(seed: int = 0) -> dict:
    keys = jax.random.split(jax.random.key(seed), 5)
    return {
        "star_state": draw_star_state(jax.random.fold_in(keys[4], 71), 0),
        "star_times": jnp.clip(-0.25 + 0.25 * jax.random.uniform(keys[1], (N,), jnp.float32) ** steps_of(keys[1], (N,), ((0, 8),), -0.2, 0.2), -0.25, 0.0),
        "masses": jnp.clip(jnp.exp(math.log(1.52587890625e-05) - 3.218876 * jax.random.uniform(keys[2], (N,), jnp.float32) ** steps_of(keys[2], (N,), ((0, 8),), -0.2, 0.2)), 6.103515488575795e-07, 1.52587890625e-05),
        "active_ids": draw_active_ids(jax.random.fold_in(keys[4], 71), 0),
    }


soften_square = 0.01
block_step = 0.0625

def predict(current, delta):
    position = current[0:3]
    velocity = current[3:6]
    acceleration = current[6:9]
    jerk_rows = current[9:12]
    new_position = position + delta * (velocity + delta * (acceleration / 2.0 + delta * jerk_rows / 6.0))
    new_velocity = velocity + delta * (acceleration + delta * jerk_rows / 2.0)
    return (new_position, new_velocity)

def pair_sums(active_pos, active_vel, field_pos, field_vel, field_mass):
    field_count = field_pos.shape[1]
    block_width = min(field_count, 1024)
    block_turns = field_count // block_width

    def one_block(turn_index, carried):
        block_start = turn_index * block_width
        block_pos = lax.dynamic_slice_in_dim(field_pos, block_start, block_width, 1)
        block_vel = lax.dynamic_slice_in_dim(field_vel, block_start, block_width, 1)
        block_mass = lax.dynamic_slice_in_dim(field_mass, block_start, block_width, 0)
        separation = block_pos[:, None, :] - active_pos[:, :, None]
        rel_vel = block_vel[:, None, :] - active_vel[:, :, None]
        soft_square = lax.optimization_barrier(jnp.sum(separation * separation, axis=0)) + soften_square
        inverse = 1.0 / jnp.sqrt(soft_square)
        weights = block_mass[None, :] * inverse * inverse * inverse
        radial = lax.optimization_barrier(jnp.sum(separation * rel_vel, axis=0))
        pull = lax.optimization_barrier(jnp.sum(weights * separation, axis=-1))
        jerk_sum = lax.optimization_barrier(jnp.sum(weights * (rel_vel - 3.0 * (radial / soft_square) * separation), axis=-1))
        potential = -lax.optimization_barrier(jnp.sum(block_mass[None, :] * inverse, axis=-1))
        return carried + jnp.concatenate([pull, jerk_sum, potential[None]], 0)
    start_value = jnp.zeros((7, active_pos.shape[1]), active_pos.dtype)
    return lax.fori_loop(0, block_turns, one_block, start_value)

def correct(previous, pair_terms, elapsed):
    old_pos = previous[0:3]
    old_vel = previous[3:6]
    old_acc = previous[6:9]
    old_jerk = previous[9:12]
    new_acc = pair_terms[0:3]
    new_jerk = pair_terms[3:6]
    new_vel = old_vel + elapsed * (old_acc + new_acc) / 2.0 + elapsed * elapsed * (old_jerk - new_jerk) / 12.0
    new_pos = old_pos + elapsed * (old_vel + new_vel) / 2.0 + elapsed * elapsed * (old_acc - new_acc) / 12.0
    return jnp.concatenate([new_pos, new_vel, new_acc, new_jerk], 0)

def reference(star_state, star_times, masses, active_ids):
    current = star_state
    star_clock = star_times
    potential_rows = []
    for step_index in range(STEPS):
        now_time = (step_index + 1) * block_step
        field_pos, field_vel = predict(current, now_time - star_clock)
        block_ids = active_ids[step_index]
        previous = current[:, block_ids]
        elapsed = now_time - star_clock[block_ids]
        active_pos, active_vel = predict(previous, elapsed)
        pair_terms = pair_sums(active_pos, active_vel, field_pos, field_vel, masses)
        refreshed = correct(previous, pair_terms, elapsed)
        potential_rows.append(pair_terms[6])
        current = current.at[:, block_ids].set(refreshed)
        star_clock = star_clock.at[block_ids].set(now_time)
    return (current, jnp.stack(potential_rows, 0))
```

```python
import functools

import jax
import jax.numpy as jnp
from jax import lax
from jax.experimental import pallas as pl
from jax.experimental.pallas import tpu as pltpu
from jax.sharding import PartitionSpec as P

soften_square = 0.01
block_step = 0.0625
LANES = 128
ROWS = 16
MESH = pl.DeviceIdType.MESH
NT = (((1,), (1,)), ((), ()))
VMEM = pl.BlockSpec(memory_space=pltpu.VMEM)
f32 = jnp.float32
bf16 = jnp.bfloat16


def split3(value):
    high = value.astype(bf16)
    rest = value - high.astype(f32)
    middle = rest.astype(bf16)
    low = (rest - middle.astype(f32)).astype(bf16)
    return high, middle, low


def sum3(stacked):
    return stacked[0:ROWS] + stacked[ROWS : 2 * ROWS] + stacked[2 * ROWS : 3 * ROWS]


def predict_rows(rows, now_time):
    delta = now_time - rows[12:13]
    pos, vel, acc, jerk = rows[0:3], rows[3:6], rows[6:9], rows[9:12]
    new_pos = pos + delta * (vel + delta * (acc / 2.0 + delta * jerk / 6.0))
    new_vel = vel + delta * (acc + delta * jerk / 2.0)
    return new_pos, new_vel


def gather_kernel(field_ref, ids_ref, out_ref, table, product):
    count = field_ref.shape[1]
    tiles = count // LANES
    for h in range(tiles):
        parts = split3(field_ref[:, h * LANES : (h + 1) * LANES])
        for p in range(3):
            table[p, h * ROWS : (h + 1) * ROWS, :] = parts[p].astype(f32)
    first = lax.axis_index("fld") * count
    width = out_ref.shape[2]

    def chunk(c, carry):
        local = ids_ref[c] - first
        high, low = local >> 7, local & (LANES - 1)
        hot = (lax.broadcasted_iota(jnp.int32, (LANES, width), 0) == low).astype(f32).astype(bf16)
        total = jnp.dot(table[0].astype(bf16), hot, preferred_element_type=f32)
        total += jnp.dot(table[1].astype(bf16), hot, preferred_element_type=f32)
        total += jnp.dot(table[2].astype(bf16), hot, preferred_element_type=f32)
        product[...] = total
        picked = jnp.zeros((ROWS, width), f32)
        for h in range(tiles):
            picked += jnp.where(high == h, product[h * ROWS : (h + 1) * ROWS, :], 0.0)
        out_ref[c] = picked
        return carry

    lax.fori_loop(0, out_ref.shape[0], chunk, 0)


def fetch_kernel(n, part_ref, out_ref, landing, gathered, send1, recv1, send2, recv2):
    act, me = lax.axis_index("act"), lax.axis_index("fld")
    barrier = pltpu.get_barrier_semaphore()
    for o in range(1, n):
        pl.semaphore_signal(barrier, inc=1, device_id=(act, lax.rem(me + o, n)), device_id_type=MESH)
    pl.semaphore_wait(barrier, n - 1)
    copies = []
    for o in range(1, n):
        peer = lax.rem(me + o, n)
        copies.append(pltpu.make_async_remote_copy(
            src_ref=part_ref.at[peer], dst_ref=landing.at[o], send_sem=send1.at[o], recv_sem=recv1.at[o],
            device_id=(act, peer), device_id_type=MESH))
        copies[-1].start()
    total = part_ref[me]
    for o in range(1, n):
        copies[o - 1].wait_recv()
        total += landing[o]
    gathered[me] = total
    again = []
    for o in range(1, n):
        peer = lax.rem(me + o, n)
        again.append(pltpu.make_async_remote_copy(
            src_ref=gathered.at[me], dst_ref=gathered.at[me], send_sem=send2.at[o], recv_sem=recv2.at[o],
            device_id=(act, peer), device_id_type=MESH))
        again[-1].start()
    for o in range(1, n):
        again[o - 1].wait_recv()
    for o in range(1, n):
        copies[o - 1].wait_send()
        again[o - 1].wait_send()
    width = part_ref.shape[2]
    for c in range(n):
        out_ref[:, c * width : (c + 1) * width] = gathered[c]


def update_field(field_in, field_out, values_ref, ids_ref, scaled):
    count = field_in.shape[1]
    tiles = count // LANES
    local = ids_ref[...] - lax.axis_index("fld") * count
    high, low = local >> 7, local & (LANES - 1)
    hot = (lax.broadcasted_iota(jnp.int32, (LANES, local.shape[1]), 0) == low).astype(f32).astype(bf16)
    parts = jnp.concatenate(split3(values_ref[...]), 0)
    for h in range(tiles):
        chosen = (high == h).astype(f32).astype(bf16)
        scaled[h * 3 * ROWS : (h + 1) * 3 * ROWS, :] = parts * chosen
    placed = lax.dot_general(scaled[...], hot, NT, preferred_element_type=f32)
    for h in range(tiles):
        fresh = sum3(placed[h * 3 * ROWS : (h + 1) * 3 * ROWS, :])
        old = field_in[:, h * LANES : (h + 1) * LANES]
        field_out[:, h * LANES : (h + 1) * LANES] = jnp.where(fresh[13:14] > 0.5, fresh, old)


def final_kernel(field_in, values_ref, ids_ref, out_ref, field, scaled):
    update_field(field_in, field, values_ref, ids_ref, scaled)
    out_ref[...] = field[0:12, :]


def pair_kernel(step, n, *refs):
    now_time = (step + 1) * block_step
    field_in, mass_ref, prev_in, column_ids = refs[:4]
    refs = refs[4:]
    values = refs[:step]
    ids = refs[step : 2 * step]
    refs = refs[2 * step :]
    sums_ref, prev_out = refs[:2]
    refs = refs[2:]
    if step:
        field = refs[0]
        points, columns, weight, second, potential, scaled = refs[1:]
        update_field(field_in, field, values[step - 1], ids[step - 1], scaled)
    else:
        field = field_in
        points, columns, weight, second, potential = refs
    count = field_in.shape[1]
    actives = prev_in.shape[1]
    previous = prev_in[...]
    for j in range(step):
        hot = (column_ids[...] == ids[j][...]).astype(f32).astype(bf16)
        parts = jnp.concatenate(split3(values[j][...]), 0)
        found = lax.dot_general(hot, parts, NT, preferred_element_type=f32)
        fresh = sum3(jnp.transpose(found))
        previous = jnp.where(fresh[13:14] > 0.5, fresh, previous)
    active_pos, active_vel = predict_rows(previous, now_time)
    pad2 = jnp.zeros((2, actives), f32)
    columns[...] = jnp.transpose(jnp.concatenate([active_pos, active_vel, pad2], 0))
    pos, vel = predict_rows(field[...], now_time)
    ones = jnp.ones((1, count), f32)
    both = jnp.concatenate([pos, vel, mass_ref[...], ones], 0)
    points[...] = both
    high = both.astype(bf16)
    low = (both - high.astype(f32)).astype(bf16)
    right = jnp.concatenate([high, low], 0)
    group = 16

    def one_group(i, carry):
        rows = pl.ds(pl.multiple_of(i * group, group), group)
        mine = [jnp.broadcast_to(columns[rows, r : r + 1], (group, LANES)) for r in range(6)]
        pot = jnp.zeros((group, LANES), f32)
        for c in range(count // LANES):
            at = slice(c * LANES, (c + 1) * LANES)
            sep = [points[r : r + 1, at] - mine[r] for r in range(3)]
            rel = [points[r : r + 1, at] - mine[r] for r in range(3, 6)]
            square = sep[0] * sep[0] + sep[1] * sep[1] + sep[2] * sep[2] + soften_square
            radial = sep[0] * rel[0] + sep[1] * rel[1] + sep[2] * rel[2]
            inverse = lax.rsqrt(square)
            inverse2 = inverse * inverse
            weighted = points[6:7, at] * inverse
            pot = pot + weighted
            w = weighted * inverse2
            weight[rows, at] = w.astype(bf16)
            second[rows, at] = (w * (inverse2 * radial)).astype(bf16)
        potential[rows, :] = pot
        return carry

    lax.fori_loop(0, actives // group, one_group, 0)
    first = jnp.transpose(lax.dot_general(weight[...], right, NT, preferred_element_type=f32))
    first = first[0:8] + first[8:16]
    other = jnp.transpose(lax.dot_general(second[...], right, NT, preferred_element_type=f32))
    other = other[0:8] + other[8:16]
    pot = -jnp.sum(jnp.transpose(potential[...]), axis=0, keepdims=True)
    pull = first[0:3] - active_pos * first[7:8]
    radial_part = other[0:3] - active_pos * other[7:8]
    jerk = first[3:6] - active_vel * first[7:8] - 3.0 * radial_part
    sums = jnp.concatenate([pull, jerk, pot, jnp.zeros((1, actives), f32)], 0)
    width = actives // n
    for c in range(n):
        sums_ref[c] = sums[:, c * width : (c + 1) * width]
        prev_out[c] = previous[:, c * width : (c + 1) * width]


def correct_rows(prev, total, now_time):
    h = now_time - prev[12:13]
    x0, v0, a0, j0 = prev[0:3], prev[3:6], prev[6:9], prev[9:12]
    a1, j1 = total[0:3], total[3:6]
    v1 = v0 + h * (a0 + a1) / 2.0 + h * h * (j0 - j1) / 12.0
    x1 = x0 + h * (v0 + v1) / 2.0 + h * h * (a0 - a1) / 12.0
    width = prev.shape[1]
    return jnp.concatenate([
        x1, v1, a1, j1, jnp.full((1, width), now_time, f32), jnp.ones((1, width), f32),
        total[6:7], jnp.zeros((1, width), f32)], 0)


def share_kernel(step, n_act, n, part_ref, prev_ref, out_ref, landing, gathered, send1, recv1, send2, recv2):
    act, me = lax.axis_index("act"), lax.axis_index("fld")
    devices = n_act * n
    index = act * n + me
    barrier = pltpu.get_barrier_semaphore()

    def place(o):
        other = lax.rem(index + o, devices)
        return (other // n, lax.rem(other, n))

    def greet(o, carry):
        pl.semaphore_signal(barrier, inc=1, device_id=place(o), device_id_type=MESH)
        return carry

    lax.fori_loop(1, devices, greet, 0)
    pl.semaphore_wait(barrier, devices - 1)
    copies = []
    for o in range(1, n):
        peer = lax.rem(me + o, n)
        copies.append(pltpu.make_async_remote_copy(
            src_ref=part_ref.at[peer], dst_ref=landing.at[o], send_sem=send1.at[o], recv_sem=recv1.at[o],
            device_id=(act, peer), device_id_type=MESH))
        copies[-1].start()
    total = part_ref[me]
    for o in range(1, n):
        copies[o - 1].wait_recv()
        total += landing[o]
    gathered[index] = correct_rows(prev_ref[me], total, (step + 1) * block_step)

    def copy(o):
        return pltpu.make_async_remote_copy(
            src_ref=gathered.at[index], dst_ref=gathered.at[index], send_sem=send2.at[o], recv_sem=recv2.at[o],
            device_id=place(o), device_id_type=MESH)

    def start(o, carry):
        copy(o).start()
        return carry

    def receive(o, carry):
        copy(o).wait_recv()
        return carry

    def sent(o, carry):
        copy(o).wait_send()
        return carry

    lax.fori_loop(1, devices, start, 0)
    lax.fori_loop(1, devices, receive, 0)
    width = part_ref.shape[2]
    for d in range(devices):
        out_ref[:, d * width : (d + 1) * width] = gathered[d]
    lax.fori_loop(1, devices, sent, 0)
    for o in range(1, n):
        copies[o - 1].wait_send()


def body(n_act, n_fld, star_state, star_times, masses, active_ids):
    count = star_state.shape[1]
    steps, listed = active_ids.shape
    actives = listed // n_act
    width = actives // n_fld
    devices = n_act * n_fld
    act = lax.axis_index("act")
    tiles = count // LANES
    field = jnp.concatenate([star_state, star_times[None], jnp.zeros((3, count), f32)], 0)
    mass = masses[None]
    mine = lax.dynamic_slice_in_dim(active_ids, act * actives, actives, 1)
    wide = steps * actives // n_fld
    params = functools.partial(pltpu.CompilerParams, vmem_limit_bytes=60 * 1024 * 1024)
    part = pl.pallas_call(
        gather_kernel,
        out_shape=jax.ShapeDtypeStruct((n_fld, ROWS, wide), f32),
        in_specs=[VMEM] * 2, out_specs=VMEM,
        scratch_shapes=[pltpu.VMEM((3, tiles * ROWS, LANES), f32), pltpu.VMEM((tiles * ROWS, wide), f32)],
        compiler_params=params(), name="gather",
    )(field, mine.reshape(n_fld, 1, wide))
    dma = pltpu.SemaphoreType.DMA
    fetched = pl.pallas_call(
        functools.partial(fetch_kernel, n_fld),
        out_shape=jax.ShapeDtypeStruct((ROWS, steps * actives), f32),
        in_specs=[VMEM], out_specs=VMEM,
        scratch_shapes=[pltpu.VMEM((n_fld, ROWS, wide), f32)] * 2 + [dma((n_fld,))] * 4,
        compiler_params=params(collective_id=0, has_side_effects=True), name="fetch",
    )(part)
    history, id_rows = [], []
    columns = mine.T
    for k in range(steps):
        outs = [jax.ShapeDtypeStruct((n_fld, 8, width), f32), jax.ShapeDtypeStruct((n_fld, ROWS, width), f32)]
        scratch = [
            pltpu.VMEM((8, count), f32), pltpu.VMEM((actives, 8), f32),
            pltpu.VMEM((actives, count), bf16), pltpu.VMEM((actives, count), bf16),
            pltpu.VMEM((actives, LANES), f32)]
        if k:
            outs.append(jax.ShapeDtypeStruct((ROWS, count), f32))
            scratch.append(pltpu.VMEM((tiles * 3 * ROWS, listed), bf16))
        results = pl.pallas_call(
            functools.partial(pair_kernel, k, n_fld),
            out_shape=outs, in_specs=[VMEM] * (4 + 2 * k), out_specs=[VMEM] * len(outs),
            scratch_shapes=scratch, compiler_params=params(), name=f"pairs{k}",
        )(field, mass, fetched[:, k * actives : (k + 1) * actives], columns[:, k : k + 1], *history, *id_rows)
        if k:
            field = results[2]
        values = pl.pallas_call(
            functools.partial(share_kernel, k, n_act, n_fld),
            out_shape=jax.ShapeDtypeStruct((ROWS, listed), f32),
            in_specs=[VMEM] * 2, out_specs=VMEM,
            scratch_shapes=[
                pltpu.VMEM((n_fld, 8, width), f32), pltpu.VMEM((devices, ROWS, width), f32),
                dma((n_fld,)), dma((n_fld,)), dma((devices,)), dma((devices,))],
            compiler_params=params(collective_id=k + 1, has_side_effects=True), name=f"share{k}",
        )(results[0], results[1])
        history.append(values)
        id_rows.append(active_ids[k : k + 1])
    final = pl.pallas_call(
        final_kernel,
        out_shape=jax.ShapeDtypeStruct((12, count), f32),
        in_specs=[VMEM] * 3, out_specs=VMEM,
        scratch_shapes=[pltpu.VMEM((ROWS, count), f32), pltpu.VMEM((tiles * 3 * ROWS, listed), bf16)],
        compiler_params=params(), name="final",
    )(field, history[-1], id_rows[-1])
    potentials = jnp.stack([lax.dynamic_slice_in_dim(v[14], act * actives, actives, 0) for v in history], 0)
    return final, potentials


def solution(mesh):
    in_specs = (P(None, "fld"), P("fld"), P("fld"), P())
    out_specs = (P(None, "fld"), P(None, "act"))
    run = functools.partial(body, mesh.shape["act"], mesh.shape["fld"])
    return jax.shard_map(run, mesh=mesh, in_specs=in_specs, out_specs=out_specs, check_vma=False)
```

```python
import functools

import jax
import jax.numpy as jnp
from jax import lax
from jax.experimental import pallas as pl
from jax.experimental.pallas import tpu as pltpu
from jax.sharding import PartitionSpec as P

soften_square = 0.01
block_step = 0.0625
LANES = 128
CHUNK = 256
SHIFT = 8
ROWS = 16
MESH = pl.DeviceIdType.MESH
NT = (((1,), (1,)), ((), ()))
VMEM = pl.BlockSpec(memory_space=pltpu.VMEM)
f32 = jnp.float32
bf16 = jnp.bfloat16


def split3(value):
    high = value.astype(bf16)
    rest = value - high.astype(f32)
    middle = rest.astype(bf16)
    low = (rest - middle.astype(f32)).astype(bf16)
    return high, middle, low


def sum3(stacked):
    return stacked[0:ROWS] + stacked[ROWS : 2 * ROWS] + stacked[2 * ROWS : 3 * ROWS]


def predict_rows(rows, now_time):
    delta = now_time - rows[12:13]
    pos, vel, acc, jerk = rows[0:3], rows[3:6], rows[6:9], rows[9:12]
    new_pos = pos + delta * (vel + delta * (acc / 2.0 + delta * jerk / 6.0))
    new_vel = vel + delta * (acc + delta * jerk / 2.0)
    return new_pos, new_vel


def gather_kernel(state_ref, times_ref, ids_ref, out_ref, field_ref, table, product):
    count = state_ref.shape[1]
    tiles = count // CHUNK
    field_ref[...] = jnp.concatenate([state_ref[...], times_ref[...], jnp.zeros((3, count), f32)], 0)
    for h in range(tiles):
        parts = split3(field_ref[:, h * CHUNK : (h + 1) * CHUNK])
        for p in range(3):
            table[p, h * ROWS : (h + 1) * ROWS, :] = parts[p]
    first = lax.axis_index("fld") * count
    width = out_ref.shape[2]

    def chunk(c, carry):
        local = ids_ref[c] - first
        high, low = local >> SHIFT, local & (CHUNK - 1)
        hot = (lax.broadcasted_iota(jnp.int32, (CHUNK, width), 0) == low).astype(f32).astype(bf16)
        total = jnp.dot(table[0], hot, preferred_element_type=f32)
        total += jnp.dot(table[1], hot, preferred_element_type=f32)
        total += jnp.dot(table[2], hot, preferred_element_type=f32)
        product[...] = total
        picked = jnp.zeros((ROWS, width), f32)
        for h in range(tiles):
            picked += jnp.where(high == h, product[h * ROWS : (h + 1) * ROWS, :], 0.0)
        out_ref[c] = picked
        return carry

    lax.fori_loop(0, out_ref.shape[0], chunk, 0)


def fetch_kernel(n, part_ref, out_ref, landing, gathered, send1, recv1, send2, recv2):
    act, me = lax.axis_index("act"), lax.axis_index("fld")
    barrier = pltpu.get_barrier_semaphore()
    for o in range(1, n):
        pl.semaphore_signal(barrier, inc=1, device_id=(act, lax.rem(me + o, n)), device_id_type=MESH)
    pl.semaphore_wait(barrier, n - 1)
    copies = []
    for o in range(1, n):
        peer = lax.rem(me + o, n)
        copies.append(pltpu.make_async_remote_copy(
            src_ref=part_ref.at[peer], dst_ref=landing.at[o], send_sem=send1.at[o], recv_sem=recv1.at[o],
            device_id=(act, peer), device_id_type=MESH))
        copies[-1].start()
    total = part_ref[me]
    for o in range(1, n):
        copies[o - 1].wait_recv()
        total += landing[o]
    gathered[me] = total
    again = []
    for o in range(1, n):
        peer = lax.rem(me + o, n)
        again.append(pltpu.make_async_remote_copy(
            src_ref=gathered.at[me], dst_ref=gathered.at[me], send_sem=send2.at[o], recv_sem=recv2.at[o],
            device_id=(act, peer), device_id_type=MESH))
        again[-1].start()
    for o in range(1, n):
        again[o - 1].wait_recv()
    for o in range(1, n):
        copies[o - 1].wait_send()
        again[o - 1].wait_send()
    width = part_ref.shape[2]
    for c in range(n):
        out_ref[:, c * width : (c + 1) * width] = gathered[c]


def update_field(field_in, field_out, values_ref, ids, scaled):
    count = field_in.shape[1]
    tiles = count // CHUNK
    local = ids - lax.axis_index("fld") * count
    high, low = local >> SHIFT, local & (CHUNK - 1)
    hot = (lax.broadcasted_iota(jnp.int32, (CHUNK, local.shape[1]), 0) == low).astype(f32).astype(bf16)
    parts = jnp.concatenate(split3(values_ref[...]), 0)
    for h in range(tiles):
        chosen = (high == h).astype(f32).astype(bf16)
        scaled[h * 3 * ROWS : (h + 1) * 3 * ROWS, :] = parts * chosen
    placed = lax.dot_general(scaled[...], hot, NT, preferred_element_type=f32)
    for h in range(tiles):
        fresh = sum3(placed[h * 3 * ROWS : (h + 1) * 3 * ROWS, :])
        old = field_in[:, h * CHUNK : (h + 1) * CHUNK]
        field_out[:, h * CHUNK : (h + 1) * CHUNK] = jnp.where(fresh[13:14] > 0.5, fresh, old)


def final_kernel(field_in, values_ref, ids_ref, out_ref, field, scaled):
    update_field(field_in, field, values_ref, ids_ref[ids_ref.shape[0] - 1 :, :], scaled)
    out_ref[...] = field[0:12, :]


def pair_kernel(step, n, *refs):
    now_time = (step + 1) * block_step
    field_in, mass_ref, prev_in, column_ids, ids = refs[:5]
    refs = refs[5:]
    values = refs[:step]
    refs = refs[step:]
    sums_ref, prev_out = refs[:2]
    refs = refs[2:]
    if step:
        field = refs[0]
        points, right, mine, even, odd, sums, potential, scaled = refs[1:]
        update_field(field_in, field, values[step - 1], ids[step - 1 : step, :], scaled)
    else:
        field = field_in
        points, right, mine, even, odd, sums, potential = refs
    chunks = points.shape[0]
    parts_of, half = mine.shape[1], mine.shape[2]
    actives = parts_of * half
    previous = prev_in[:, step * actives : (step + 1) * actives]
    for j in range(step):
        hot = (column_ids[:, step : step + 1] == ids[j : j + 1, :]).astype(f32).astype(bf16)
        parts = jnp.concatenate(split3(values[j][...]), 0)
        found = lax.dot_general(hot, parts, NT, preferred_element_type=f32)
        fresh = sum3(jnp.transpose(found))
        previous = jnp.where(fresh[13:14] > 0.5, fresh, previous)
    active_pos, active_vel = predict_rows(previous, now_time)
    pad2 = jnp.zeros((2, actives), f32)
    columns = jnp.transpose(jnp.concatenate([active_pos, active_vel, pad2], 0))
    for r in range(6):
        for p in range(parts_of):
            mine[r, p] = jnp.broadcast_to(columns[p * half : (p + 1) * half, r : r + 1], (half, LANES))
    pos, vel = predict_rows(field[...], now_time)
    both = jnp.concatenate([pos, vel, mass_ref[...], jnp.ones((1, pos.shape[1]), f32)], 0)
    high = both.astype(bf16)
    low = (both - high.astype(f32)).astype(bf16)
    split = jnp.concatenate([high, low], 0)
    for c in range(chunks):
        points[c] = both[:, c * CHUNK : (c + 1) * CHUNK]
        right[c] = split[:, c * CHUNK : (c + 1) * CHUNK]
    group = 16
    sums[...] = jnp.zeros_like(sums)
    potential[...] = jnp.zeros_like(potential)
    odd[...] = jnp.zeros_like(odd)

    def fill(buffer, turn):
        p, c = turn // chunks, lax.rem(turn, chunks)
        for g in range(half // group):
            rows = slice(g * group, (g + 1) * group)
            pot = potential[p, rows, :]
            for t in range(CHUNK // LANES):
                at = slice(t * LANES, (t + 1) * LANES)
                sep = [points[c, r : r + 1, at] - mine[r, p, rows, :] for r in range(3)]
                rel = [points[c, r : r + 1, at] - mine[r, p, rows, :] for r in range(3, 6)]
                square = sep[0] * sep[0] + sep[1] * sep[1] + sep[2] * sep[2] + soften_square
                radial = sep[0] * rel[0] + sep[1] * rel[1] + sep[2] * rel[2]
                inverse = lax.rsqrt(square)
                inverse2 = inverse * inverse
                weighted = points[c, 6:7, at] * inverse
                pot = pot + weighted
                w = weighted * inverse2
                buffer[rows, at] = w.astype(bf16)
                buffer[half + g * group : half + (g + 1) * group, at] = (w * (inverse2 * radial)).astype(bf16)
            potential[p, rows, :] = pot

    def drain(buffer, turn):
        p, c = turn // chunks, lax.rem(turn, chunks)
        sums[p] += lax.dot_general(buffer[...], right[c], NT, preferred_element_type=f32)

    def two(i, carry):
        fill(even, 2 * i)
        drain(odd, jnp.maximum(2 * i - 1, 0))
        fill(odd, 2 * i + 1)
        drain(even, 2 * i)
        return carry

    turns = parts_of * chunks
    lax.fori_loop(0, turns // 2, two, 0)
    drain(odd, turns - 1)
    firsts, others, pots = [], [], []
    for p in range(parts_of):
        both = jnp.transpose(sums[p])
        both = both[0:8] + both[8:16]
        firsts.append(both[:, 0:half])
        others.append(both[:, half:])
        pots.append(-jnp.sum(jnp.transpose(potential[p]), axis=0, keepdims=True))
    first, other = jnp.concatenate(firsts, 1), jnp.concatenate(others, 1)
    pot = jnp.concatenate(pots, 1)
    pull = first[0:3] - active_pos * first[7:8]
    radial_part = other[0:3] - active_pos * other[7:8]
    jerk = first[3:6] - active_vel * first[7:8] - 3.0 * radial_part
    total = jnp.concatenate([pull, jerk, pot, jnp.zeros((1, actives), f32)], 0)
    width = actives // n
    for c in range(n):
        sums_ref[c] = total[:, c * width : (c + 1) * width]
        prev_out[c] = previous[:, c * width : (c + 1) * width]


def correct_rows(prev, total, now_time):
    h = now_time - prev[12:13]
    x0, v0, a0, j0 = prev[0:3], prev[3:6], prev[6:9], prev[9:12]
    a1, j1 = total[0:3], total[3:6]
    v1 = v0 + h * (a0 + a1) / 2.0 + h * h * (j0 - j1) / 12.0
    x1 = x0 + h * (v0 + v1) / 2.0 + h * h * (a0 - a1) / 12.0
    width = prev.shape[1]
    return jnp.concatenate([
        x1, v1, a1, j1, jnp.full((1, width), now_time, f32), jnp.ones((1, width), f32),
        total[6:7], jnp.zeros((1, width), f32)], 0)


def share_kernel(step, n_act, n, part_ref, prev_ref, out_ref, pot_ref, landing, gathered, send1, recv1, send2, recv2):
    act, me = lax.axis_index("act"), lax.axis_index("fld")
    devices = n_act * n
    index = act * n + me
    barrier = pltpu.get_barrier_semaphore()

    def place(o):
        other = lax.rem(index + o, devices)
        return (other // n, lax.rem(other, n))

    def greet(o, carry):
        pl.semaphore_signal(barrier, inc=1, device_id=place(o), device_id_type=MESH)
        return carry

    lax.fori_loop(1, devices, greet, 0)
    pl.semaphore_wait(barrier, devices - 1)
    copies = []
    for o in range(1, n):
        peer = lax.rem(me + o, n)
        copies.append(pltpu.make_async_remote_copy(
            src_ref=part_ref.at[peer], dst_ref=landing.at[o], send_sem=send1.at[o], recv_sem=recv1.at[o],
            device_id=(act, peer), device_id_type=MESH))
        copies[-1].start()
    total = part_ref[me]
    for o in range(1, n):
        copies[o - 1].wait_recv()
        total += landing[o]
    fresh = correct_rows(prev_ref[me], total, (step + 1) * block_step)
    gathered[index] = jnp.concatenate([fresh[0:8], fresh[8:16]], 1)

    def copy(o):
        return pltpu.make_async_remote_copy(
            src_ref=gathered.at[index], dst_ref=gathered.at[index], send_sem=send2.at[o], recv_sem=recv2.at[o],
            device_id=place(o), device_id_type=MESH)

    def start(o, carry):
        copy(o).start()
        return carry

    def receive(o, carry):
        copy(o).wait_recv()
        return carry

    def sent(o, carry):
        copy(o).wait_send()
        return carry

    lax.fori_loop(1, devices, start, 0)
    lax.fori_loop(1, devices, receive, 0)
    width = part_ref.shape[2]
    for d in range(devices):
        packed = gathered[d]
        out_ref[0:8, d * width : (d + 1) * width] = packed[:, 0:width]
        out_ref[8:16, d * width : (d + 1) * width] = packed[:, width:]
    for c in range(n):
        pot_ref[:, c * width : (c + 1) * width] = gathered[act * n + c][6:7, width:]
    lax.fori_loop(1, devices, sent, 0)
    for o in range(1, n):
        copies[o - 1].wait_send()


def body(n_act, n_fld, star_state, star_times, masses, active_ids):
    count = star_state.shape[1]
    steps, listed = active_ids.shape
    actives = listed // n_act
    width = actives // n_fld
    devices = n_act * n_fld
    act = lax.axis_index("act")
    tiles = count // CHUNK
    mine = lax.dynamic_slice_in_dim(active_ids, act * actives, actives, 1)
    wide = steps * actives // n_fld
    half = min(actives, 256)
    parts_of = actives // half
    params = functools.partial(pltpu.CompilerParams, vmem_limit_bytes=60 * 1024 * 1024)
    part, field = pl.pallas_call(
        gather_kernel,
        out_shape=[jax.ShapeDtypeStruct((n_fld, ROWS, wide), f32), jax.ShapeDtypeStruct((ROWS, count), f32)],
        in_specs=[VMEM] * 3, out_specs=[VMEM] * 2,
        scratch_shapes=[pltpu.VMEM((3, tiles * ROWS, CHUNK), bf16), pltpu.VMEM((tiles * ROWS, wide), f32)],
        compiler_params=params(), name="gather",
    )(star_state, star_times[None], mine.reshape(n_fld, 1, wide))
    dma = pltpu.SemaphoreType.DMA
    fetched = pl.pallas_call(
        functools.partial(fetch_kernel, n_fld),
        out_shape=jax.ShapeDtypeStruct((ROWS, steps * actives), f32),
        in_specs=[VMEM], out_specs=VMEM,
        scratch_shapes=[pltpu.VMEM((n_fld, ROWS, wide), f32)] * 2 + [dma((n_fld,))] * 4,
        compiler_params=params(collective_id=0, has_side_effects=True), name="fetch",
    )(part)
    history, pots = [], []
    columns = mine.T
    for k in range(steps):
        outs = [jax.ShapeDtypeStruct((n_fld, 8, width), f32), jax.ShapeDtypeStruct((n_fld, ROWS, width), f32)]
        scratch = [
            pltpu.VMEM((tiles, 8, CHUNK), f32), pltpu.VMEM((tiles, 16, CHUNK), bf16),
            pltpu.VMEM((6, parts_of, half, LANES), f32),
            pltpu.VMEM((2 * half, CHUNK), bf16), pltpu.VMEM((2 * half, CHUNK), bf16),
            pltpu.VMEM((parts_of, 2 * half, 16), f32), pltpu.VMEM((parts_of, half, LANES), f32)]
        if k:
            outs.append(jax.ShapeDtypeStruct((ROWS, count), f32))
            scratch.append(pltpu.VMEM((tiles * 3 * ROWS, listed), bf16))
        results = pl.pallas_call(
            functools.partial(pair_kernel, k, n_fld),
            out_shape=outs, in_specs=[VMEM] * (5 + k), out_specs=[VMEM] * len(outs),
            scratch_shapes=scratch, compiler_params=params(), name=f"pairs{k}",
        )(field, masses[None], fetched, columns, active_ids, *history)
        if k:
            field = results[2]
        values, pot = pl.pallas_call(
            functools.partial(share_kernel, k, n_act, n_fld),
            out_shape=[jax.ShapeDtypeStruct((ROWS, listed), f32), jax.ShapeDtypeStruct((1, actives), f32)],
            in_specs=[VMEM] * 2, out_specs=[VMEM] * 2,
            scratch_shapes=[
                pltpu.VMEM((n_fld, 8, width), f32), pltpu.VMEM((devices, 8, 2 * width), f32),
                dma((n_fld,)), dma((n_fld,)), dma((devices,)), dma((devices,))],
            compiler_params=params(collective_id=k + 1, has_side_effects=True), name=f"share{k}",
        )(results[0], results[1])
        history.append(values)
        pots.append(pot)
    final = pl.pallas_call(
        final_kernel,
        out_shape=jax.ShapeDtypeStruct((12, count), f32),
        in_specs=[VMEM] * 3, out_specs=VMEM,
        scratch_shapes=[pltpu.VMEM((ROWS, count), f32), pltpu.VMEM((tiles * 3 * ROWS, listed), bf16)],
        compiler_params=params(), name="final",
    )(field, history[-1], active_ids)
    return final, jnp.concatenate(pots, 0)


def solution(mesh):
    in_specs = (P(None, "fld"), P("fld"), P("fld"), P())
    out_specs = (P(None, "fld"), P(None, "act"))
    run = functools.partial(body, mesh.shape["act"], mesh.shape["fld"])
    return jax.shard_map(run, mesh=mesh, in_specs=in_specs, out_specs=out_specs, check_vma=False)
```

```python
import functools

import jax
import jax.numpy as jnp
from jax import lax
from jax.experimental import pallas as pl
from jax.experimental.pallas import tpu as pltpu
from jax.sharding import PartitionSpec as P

soften_square = 0.01
block_step = 0.0625
LANES = 128
CHUNK = 256
SHIFT = 8
ROWS = 16
MESH = pl.DeviceIdType.MESH
NT = (((1,), (1,)), ((), ()))
VMEM = pl.BlockSpec(memory_space=pltpu.VMEM)
f32 = jnp.float32
bf16 = jnp.bfloat16


def split3(value):
    high = value.astype(bf16)
    rest = value - high.astype(f32)
    middle = rest.astype(bf16)
    low = (rest - middle.astype(f32)).astype(bf16)
    return high, middle, low


def sum3(stacked):
    return stacked[0:ROWS] + stacked[ROWS : 2 * ROWS] + stacked[2 * ROWS : 3 * ROWS]


def predict_rows(rows, now_time):
    delta = now_time - rows[12:13]
    pos, vel, acc, jerk = rows[0:3], rows[3:6], rows[6:9], rows[9:12]
    new_pos = pos + delta * (vel + delta * (acc / 2.0 + delta * jerk / 6.0))
    new_vel = vel + delta * (acc + delta * jerk / 2.0)
    return new_pos, new_vel


def gather_kernel(state_ref, times_ref, ids_ref, out_ref, field_ref, table, product):
    count = state_ref.shape[1]
    tiles = count // CHUNK
    field_ref[...] = jnp.concatenate([state_ref[...], times_ref[...], jnp.zeros((3, count), f32)], 0)
    for h in range(tiles):
        parts = split3(field_ref[:, h * CHUNK : (h + 1) * CHUNK])
        for p in range(3):
            table[p, h * ROWS : (h + 1) * ROWS, :] = parts[p]
    first = lax.axis_index("fld") * count
    width = out_ref.shape[2]

    def chunk(c, carry):
        local = ids_ref[c] - first
        high, low = local >> SHIFT, local & (CHUNK - 1)
        hot = (lax.broadcasted_iota(jnp.int32, (CHUNK, width), 0) == low).astype(f32).astype(bf16)
        total = jnp.dot(table[0], hot, preferred_element_type=f32)
        total += jnp.dot(table[1], hot, preferred_element_type=f32)
        total += jnp.dot(table[2], hot, preferred_element_type=f32)
        product[...] = total
        picked = jnp.zeros((ROWS, width), f32)
        for h in range(tiles):
            picked += jnp.where(high == h, product[h * ROWS : (h + 1) * ROWS, :], 0.0)
        out_ref[c] = picked
        return carry

    lax.fori_loop(0, out_ref.shape[0], chunk, 0)


def fetch_kernel(n, part_ref, out_ref, landing, gathered, send1, recv1, send2, recv2):
    act, me = lax.axis_index("act"), lax.axis_index("fld")
    barrier = pltpu.get_barrier_semaphore()
    for o in range(1, n):
        pl.semaphore_signal(barrier, inc=1, device_id=(act, lax.rem(me + o, n)), device_id_type=MESH)
    pl.semaphore_wait(barrier, n - 1)
    copies = []
    for o in range(1, n):
        peer = lax.rem(me + o, n)
        copies.append(pltpu.make_async_remote_copy(
            src_ref=part_ref.at[peer], dst_ref=landing.at[o], send_sem=send1.at[o], recv_sem=recv1.at[o],
            device_id=(act, peer), device_id_type=MESH))
        copies[-1].start()
    total = part_ref[me]
    for o in range(1, n):
        copies[o - 1].wait_recv()
        total += landing[o]
    gathered[me] = total
    again = []
    for o in range(1, n):
        peer = lax.rem(me + o, n)
        again.append(pltpu.make_async_remote_copy(
            src_ref=gathered.at[me], dst_ref=gathered.at[me], send_sem=send2.at[o], recv_sem=recv2.at[o],
            device_id=(act, peer), device_id_type=MESH))
        again[-1].start()
    for o in range(1, n):
        again[o - 1].wait_recv()
    for o in range(1, n):
        copies[o - 1].wait_send()
        again[o - 1].wait_send()
    width = part_ref.shape[2]
    for c in range(n):
        out_ref[:, c * width : (c + 1) * width] = gathered[c]


def update_field(field_in, field_out, values_ref, ids, scaled):
    count = field_in.shape[1]
    tiles = count // CHUNK
    local = ids - lax.axis_index("fld") * count
    high, low = local >> SHIFT, local & (CHUNK - 1)
    hot = (lax.broadcasted_iota(jnp.int32, (CHUNK, local.shape[1]), 0) == low).astype(f32).astype(bf16)
    parts = jnp.concatenate(split3(values_ref[...]), 0)
    for h in range(tiles):
        chosen = (high == h).astype(f32).astype(bf16)
        scaled[h * 3 * ROWS : (h + 1) * 3 * ROWS, :] = parts * chosen
    placed = lax.dot_general(scaled[...], hot, NT, preferred_element_type=f32)
    for h in range(tiles):
        fresh = sum3(placed[h * 3 * ROWS : (h + 1) * 3 * ROWS, :])
        old = field_in[:, h * CHUNK : (h + 1) * CHUNK]
        field_out[:, h * CHUNK : (h + 1) * CHUNK] = jnp.where(fresh[13:14] > 0.5, fresh, old)


def final_kernel(field_in, values_ref, ids_ref, out_ref, field, scaled):
    update_field(field_in, field, values_ref, ids_ref[ids_ref.shape[0] - 1 :, :], scaled)
    out_ref[...] = field[0:12, :]


def pair_kernel(step, n, *refs):
    now_time = (step + 1) * block_step
    field_in, mass_ref, prev_in, column_ids, ids = refs[:5]
    refs = refs[5:]
    values = refs[:step]
    refs = refs[step:]
    sums_ref, prev_out = refs[:2]
    refs = refs[2:]
    if step:
        field = refs[0]
        points, right, mine, even, odd, sums, potential, scaled = refs[1:]
        update_field(field_in, field, values[step - 1], ids[step - 1 : step, :], scaled)
    else:
        field = field_in
        points, right, mine, even, odd, sums, potential = refs
    chunks = points.shape[0]
    parts_of, half = mine.shape[1], mine.shape[2]
    actives = parts_of * half
    previous = prev_in[:, step * actives : (step + 1) * actives]
    for j in range(step):
        hot = (column_ids[:, step : step + 1] == ids[j : j + 1, :]).astype(f32).astype(bf16)
        parts = jnp.concatenate(split3(values[j][...]), 0)
        found = lax.dot_general(hot, parts, NT, preferred_element_type=f32)
        fresh = sum3(jnp.transpose(found))
        previous = jnp.where(fresh[13:14] > 0.5, fresh, previous)
    active_pos, active_vel = predict_rows(previous, now_time)
    pad2 = jnp.zeros((2, actives), f32)
    columns = jnp.transpose(jnp.concatenate([active_pos, active_vel, pad2], 0))
    for r in range(6):
        for p in range(parts_of):
            mine[r, p] = jnp.broadcast_to(columns[p * half : (p + 1) * half, r : r + 1], (half, LANES))
    pos, vel = predict_rows(field[...], now_time)
    both = jnp.concatenate([pos, vel, mass_ref[...], jnp.ones((1, pos.shape[1]), f32)], 0)
    high = both.astype(bf16)
    low = (both - high.astype(f32)).astype(bf16)
    split = jnp.concatenate([high, low], 0)
    for c in range(chunks):
        points[c] = both[:, c * CHUNK : (c + 1) * CHUNK]
        right[c] = split[:, c * CHUNK : (c + 1) * CHUNK]
    group = 16
    sums[...] = jnp.zeros_like(sums)
    potential[...] = jnp.zeros_like(potential)
    odd[...] = jnp.zeros_like(odd)

    def fill(buffer, turn):
        p, c = turn // chunks, lax.rem(turn, chunks)
        for g in range(half // group):
            rows = slice(g * group, (g + 1) * group)
            pot = potential[p, rows, :]
            for t in range(CHUNK // LANES):
                at = slice(t * LANES, (t + 1) * LANES)
                sep = [points[c, r : r + 1, at] - mine[r, p, rows, :] for r in range(3)]
                rel = [points[c, r : r + 1, at] - mine[r, p, rows, :] for r in range(3, 6)]
                square = sep[0] * sep[0] + sep[1] * sep[1] + sep[2] * sep[2] + soften_square
                radial = sep[0] * rel[0] + sep[1] * rel[1] + sep[2] * rel[2]
                inverse = lax.rsqrt(square)
                inverse2 = inverse * inverse
                weighted = points[c, 6:7, at] * inverse
                pot = pot + weighted
                w = weighted * inverse2
                buffer[rows, at] = w.astype(bf16)
                buffer[half + g * group : half + (g + 1) * group, at] = (w * (inverse2 * radial)).astype(bf16)
            potential[p, rows, :] = pot

    def drain(buffer, turn):
        p, c = turn // chunks, lax.rem(turn, chunks)
        sums[p] += lax.dot_general(buffer[...], right[c], NT, preferred_element_type=f32)

    turns = parts_of * chunks

    def two(i, carry):
        fill(even, 2 * i)
        drain(odd, lax.rem(2 * i - 1 + turns, turns))
        fill(odd, 2 * i + 1)
        drain(even, 2 * i)
        return carry

    lax.fori_loop(0, turns // 2, two, 0)
    drain(odd, turns - 1)
    firsts, others, pots = [], [], []
    for p in range(parts_of):
        both = jnp.transpose(sums[p])
        both = both[0:8] + both[8:16]
        firsts.append(both[:, 0:half])
        others.append(both[:, half:])
        pots.append(-jnp.sum(jnp.transpose(potential[p]), axis=0, keepdims=True))
    first, other = jnp.concatenate(firsts, 1), jnp.concatenate(others, 1)
    pot = jnp.concatenate(pots, 1)
    pull = first[0:3] - active_pos * first[7:8]
    radial_part = other[0:3] - active_pos * other[7:8]
    jerk = first[3:6] - active_vel * first[7:8] - 3.0 * radial_part
    total = jnp.concatenate([pull, jerk, pot, jnp.zeros((1, actives), f32)], 0)
    width = actives // n
    for c in range(n):
        sums_ref[c] = total[:, c * width : (c + 1) * width]
        prev_out[c] = previous[:, c * width : (c + 1) * width]


def correct_rows(prev, total, now_time):
    h = now_time - prev[12:13]
    x0, v0, a0, j0 = prev[0:3], prev[3:6], prev[6:9], prev[9:12]
    a1, j1 = total[0:3], total[3:6]
    v1 = v0 + h * (a0 + a1) / 2.0 + h * h * (j0 - j1) / 12.0
    x1 = x0 + h * (v0 + v1) / 2.0 + h * h * (a0 - a1) / 12.0
    width = prev.shape[1]
    return jnp.concatenate([
        x1, v1, a1, j1, jnp.full((1, width), now_time, f32), jnp.ones((1, width), f32),
        total[6:7], jnp.zeros((1, width), f32)], 0)


def share_rows(compute, step, n_act, n, part_ref, prev_ref, out_ref, pot_ref, landing, gathered, send1, recv1, send2, recv2):
    act, me = lax.axis_index("act"), lax.axis_index("fld")
    devices = n_act * n
    index = act * n + me
    barrier = pltpu.get_barrier_semaphore()

    def place(o):
        other = lax.rem(index + o, devices)
        return (other // n, lax.rem(other, n))

    def greet(o, carry):
        pl.semaphore_signal(barrier, inc=1, device_id=place(o), device_id_type=MESH)
        return carry

    lax.fori_loop(1, devices, greet, 0)
    compute()
    pl.semaphore_wait(barrier, devices - 1)
    copies = []
    for o in range(1, n):
        peer = lax.rem(me + o, n)
        copies.append(pltpu.make_async_remote_copy(
            src_ref=part_ref.at[peer], dst_ref=landing.at[o], send_sem=send1.at[o], recv_sem=recv1.at[o],
            device_id=(act, peer), device_id_type=MESH))
        copies[-1].start()
    total = part_ref[me]
    for o in range(1, n):
        copies[o - 1].wait_recv()
        total += landing[o]
    fresh = correct_rows(prev_ref[me], total, (step + 1) * block_step)
    gathered[index] = jnp.concatenate([fresh[0:8], fresh[8:16]], 1)

    def copy(o):
        return pltpu.make_async_remote_copy(
            src_ref=gathered.at[index], dst_ref=gathered.at[index], send_sem=send2.at[o], recv_sem=recv2.at[o],
            device_id=place(o), device_id_type=MESH)

    def start(o, carry):
        copy(o).start()
        return carry

    def receive(o, carry):
        copy(o).wait_recv()
        return carry

    def sent(o, carry):
        copy(o).wait_send()
        return carry

    lax.fori_loop(1, devices, start, 0)
    lax.fori_loop(1, devices, receive, 0)
    width = part_ref.shape[2]
    for d in range(devices):
        packed = gathered[d]
        out_ref[0:8, d * width : (d + 1) * width] = packed[:, 0:width]
        out_ref[8:16, d * width : (d + 1) * width] = packed[:, width:]
    for c in range(n):
        pot_ref[:, c * width : (c + 1) * width] = gathered[act * n + c][6:7, width:]
    lax.fori_loop(1, devices, sent, 0)
    for o in range(1, n):
        copies[o - 1].wait_send()


def step_kernel(step, n_act, n, *refs):
    inputs, refs = refs[: 5 + step], refs[5 + step :]
    out_ref, pot_ref = refs[:2]
    kept, refs = refs[2 : 2 + (step > 0)], refs[2 + (step > 0) :]
    part, prev = refs[:2]
    exchange, scratch = refs[2:8], refs[8:]

    def compute():
        pair_kernel(step, n, *inputs, part, prev, *kept, *scratch)

    share_rows(compute, step, n_act, n, part, prev, out_ref, pot_ref, *exchange)


def body(n_act, n_fld, star_state, star_times, masses, active_ids):
    count = star_state.shape[1]
    steps, listed = active_ids.shape
    actives = listed // n_act
    width = actives // n_fld
    devices = n_act * n_fld
    act = lax.axis_index("act")
    tiles = count // CHUNK
    mine = lax.dynamic_slice_in_dim(active_ids, act * actives, actives, 1)
    wide = steps * actives // n_fld
    half = min(actives, 256)
    parts_of = actives // half
    params = functools.partial(pltpu.CompilerParams, vmem_limit_bytes=60 * 1024 * 1024)
    part, field = pl.pallas_call(
        gather_kernel,
        out_shape=[jax.ShapeDtypeStruct((n_fld, ROWS, wide), f32), jax.ShapeDtypeStruct((ROWS, count), f32)],
        in_specs=[VMEM] * 3, out_specs=[VMEM] * 2,
        scratch_shapes=[pltpu.VMEM((3, tiles * ROWS, CHUNK), bf16), pltpu.VMEM((tiles * ROWS, wide), f32)],
        compiler_params=params(), name="gather",
    )(star_state, star_times[None], mine.reshape(n_fld, 1, wide))
    dma = pltpu.SemaphoreType.DMA
    fetched = pl.pallas_call(
        functools.partial(fetch_kernel, n_fld),
        out_shape=jax.ShapeDtypeStruct((ROWS, steps * actives), f32),
        in_specs=[VMEM], out_specs=VMEM,
        scratch_shapes=[pltpu.VMEM((n_fld, ROWS, wide), f32)] * 2 + [dma((n_fld,))] * 4,
        compiler_params=params(collective_id=0, has_side_effects=True), name="fetch",
    )(part)
    history, pots = [], []
    columns = mine.T
    for k in range(steps):
        outs = [jax.ShapeDtypeStruct((ROWS, listed), f32), jax.ShapeDtypeStruct((1, actives), f32)]
        scratch = [
            pltpu.VMEM((n_fld, 8, width), f32), pltpu.VMEM((n_fld, ROWS, width), f32),
            pltpu.VMEM((n_fld, 8, width), f32), pltpu.VMEM((devices, 8, 2 * width), f32),
            dma((n_fld,)), dma((n_fld,)), dma((devices,)), dma((devices,)),
            pltpu.VMEM((tiles, 8, CHUNK), f32), pltpu.VMEM((tiles, 16, CHUNK), bf16),
            pltpu.VMEM((6, parts_of, half, LANES), f32),
            pltpu.VMEM((2 * half, CHUNK), bf16), pltpu.VMEM((2 * half, CHUNK), bf16),
            pltpu.VMEM((parts_of, 2 * half, 16), f32), pltpu.VMEM((parts_of, half, LANES), f32)]
        if k:
            outs.append(jax.ShapeDtypeStruct((ROWS, count), f32))
            scratch.append(pltpu.VMEM((tiles * 3 * ROWS, listed), bf16))
        results = pl.pallas_call(
            functools.partial(step_kernel, k, n_act, n_fld),
            out_shape=outs, in_specs=[VMEM] * (5 + k), out_specs=[VMEM] * len(outs),
            scratch_shapes=scratch, name=f"step{k}",
            compiler_params=params(collective_id=k + 1, has_side_effects=True),
        )(field, masses[None], fetched, columns, active_ids, *history)
        values, pot = results[:2]
        if k:
            field = results[2]
        history.append(values)
        pots.append(pot)
    final = pl.pallas_call(
        final_kernel,
        out_shape=jax.ShapeDtypeStruct((12, count), f32),
        in_specs=[VMEM] * 3, out_specs=VMEM,
        scratch_shapes=[pltpu.VMEM((ROWS, count), f32), pltpu.VMEM((tiles * 3 * ROWS, listed), bf16)],
        compiler_params=params(), name="final",
    )(field, history[-1], active_ids)
    return final, jnp.concatenate(pots, 0)


def solution(mesh):
    in_specs = (P(None, "fld"), P("fld"), P("fld"), P())
    out_specs = (P(None, "fld"), P(None, "act"))
    run = functools.partial(body, mesh.shape["act"], mesh.shape["fld"])
    return jax.shard_map(run, mesh=mesh, in_specs=in_specs, out_specs=out_specs, check_vma=False)
```
